512 devices in a mesh: grp: 4 (over y_hi, core), site: 128 (over y_lo, z, x).
Axes of the slice: x: 4, y: 4 (y_hi: 2, y_lo: 2; y = y_hi * 2 + y_lo), z: 16, core: 2. Of those that a mesh axis runs over, the one named last changes fastest.
Arguments:
- noise: bfloat16 [1024, 4096], P(('grp', 'site')), may hold values from -25 to 25, as said below
- sites: bfloat16 [65536, 4096], P('site'), may hold values from -25 to 25, as said below
- weights: float32 [65536], P('site'), may hold values from -2 to 2
Outputs:
- targets: bfloat16 [1024, 4096], P(('grp', 'site'))
- potentials: float32 [1024], P(('grp', 'site'))
- new_weights: float32 [65536], P('site')
The draws below stay inside these ranges and needn't reach their ends.
Inputs may be any that keep to these rules, and one draw needn't show every extreme that they name: Entries of the noise rows are finite reals. Entries of the sites are finite reals.
All inputs are finite; a program needn't handle non-finite values.
Results may differ from the reference program's by a relative error of at most 0.014.
Values may be sent and summed in bfloat16 or wider, within the bound.
No kernel may reach another device: no remote copies, remote signals or barrier semaphores. Data moves between devices by JAX's collectives and lax.ppermute only.
A program may use at most 64 MiB of HBM per device.

```python
import jax
import jax.numpy as jnp
from jax import lax

D = 4096
SITES = 65536
ROW_GRP = 256
ROWS = 1024
N_GRP = 4


def draw_sites(key, part):
    values = jnp.clip(jax.random.normal(jax.random.fold_in(key, 1), (SITES, D), jnp.float32), -6.0, 6.0)
    return values.astype(jnp.bfloat16)


def draw_noise(key, part):
    values = jnp.clip(jax.random.normal(jax.random.fold_in(key, 2), (ROWS, D), jnp.float32), -6.0, 6.0)
    return values.astype(jnp.bfloat16)


def level_of(key, shape, cuts, smallest, top_value):
    factor_of = 1.0
    for axis_at, blocks in cuts:
        draws = jax.random.uniform(jax.random.fold_in(jax.random.fold_in(key, 6), axis_at), (blocks,), jnp.float32, smallest / len(cuts), top_value / len(cuts))
        factor_of = factor_of * jnp.repeat(jnp.exp(draws), shape[axis_at] // blocks).reshape((-1,) + (1,) * (len(shape) - 1 - axis_at))
    return factor_of


def scatter_about(rng, shape, width, reach, split=(), kind=jnp.bfloat16):
    drawn = jax.random.normal(rng, shape, jnp.float32) * width
    if len(split) > 0:
        drawn = level_of(rng, shape, split, -0.22, 0.18) * drawn
    return jnp.clip(drawn, min=-reach, max=reach).astype(kind)


def setup_inputs(seed: int = 0) -> dict:
    seeds = jax.random.split(jax.random.key(seed), 4)
    return {
        "noise": draw_noise(jax.random.fold_in(seeds[3], 71), 0),
        "sites": draw_sites(jax.random.fold_in(seeds[3], 71), 0),
        "weights": scatter_about(seeds[2], (SITES,), 0.5, 2.0, ((0, 128),), jnp.float32),
    }


EPS = 0.006
ETA = 0.05


def reference(noise, sites, weights):
    sites_f = sites.astype(jnp.float32)
    half_sq = jnp.sum(sites_f * sites_f, axis=1) / (2.0 * D)
    grouped = noise.reshape(N_GRP, ROW_GRP, D)

    def one_group(block):
        inner = jnp.dot(block, sites.T, preferred_element_type=jnp.float32)
        score = weights[None, :] + (inner / D - half_sq[None, :]) / EPS
        top = jnp.max(score, axis=1)
        lse = top + jnp.log(jnp.sum(jnp.exp(score - top[:, None]), axis=1))
        probs = jnp.exp(score - lse[:, None])
        probs_b = probs.astype(jnp.bfloat16)
        tgt = jnp.dot(probs_b, sites, preferred_element_type=jnp.float32).astype(jnp.bfloat16)
        block_f = block.astype(jnp.float32)
        pot = jnp.sum(block_f * block_f, axis=1) / (2.0 * D) - EPS * (lse - jnp.log(float(SITES)))
        return tgt, pot, jnp.sum(probs, axis=0)

    tgt, pot, mass_parts = lax.map(one_group, grouped)
    mass = jnp.sum(mass_parts, axis=0)
    new_weights = weights + ETA * (1.0 - (float(SITES) / float(ROWS)) * mass)
    return tgt.reshape(ROWS, D), pot.reshape(ROWS), new_weights
```

```python
import math

import jax
import jax.numpy as jnp
import numpy as np
from jax import lax
from jax.sharding import Mesh
from jax.sharding import PartitionSpec as P

EPS = 0.006
ETA = 0.05
PLANE = ("x", "yl")
SITE = ("yl", "z", "x")
GRP = ("yh", "core")
EVERY = GRP + SITE
LANES = 128


def pieces(v):
    hi = lax.reduce_precision(v, 8, 7)
    mid = lax.reduce_precision(v - hi, 8, 7)
    low = v - hi - mid
    return [hi.astype(jnp.bfloat16), mid.astype(jnp.bfloat16), low.astype(jnp.bfloat16)]


def joined(parts):
    a, b, c = [p.astype(jnp.float32) for p in parts]
    return a + b + c


def spread(v, axes):
    return lax.all_to_all(jnp.broadcast_to(v[None], (lax.axis_size(axes),) + v.shape), axes, 0, 0, tiled=True)


def gather_rows(noise):
    rows = lax.all_gather(noise, "z", axis=0, tiled=True)
    rows = lax.all_gather(rows, "yl", axis=0, tiled=True)
    return spread(rows, "x").reshape(-1, noise.shape[1])


def shards(noise, sites, weights):
    row_dev, width = noise.shape
    n_plane, n_z = lax.axis_size(PLANE), lax.axis_size("z")
    col = n_z * row_dev
    n_sites = sites.shape[0] * lax.axis_size(SITE)
    n_rows = row_dev * lax.axis_size(EVERY)
    sites_f = sites.astype(jnp.float32)
    half_sq = jnp.sum(sites_f * sites_f, axis=1) / (2.0 * width)
    rows = gather_rows(noise)
    inner = lax.dot_general(rows, sites, (((1,), (1,)), ((), ())), preferred_element_type=jnp.float32)
    score = weights[None, :] + (inner / width - half_sq[None, :]) / EPS
    top = jnp.max(score, axis=1)
    part = jnp.exp(score - top[:, None])
    total = jnp.sum(part, axis=1)
    near = jnp.dot(part.astype(jnp.bfloat16), sites, preferred_element_type=jnp.float32)

    stats = jnp.stack(pieces(top) + pieces(total), axis=1)
    stats = jnp.pad(stats, ((0, 0), (0, LANES - 6)))
    send = jnp.concatenate([near.astype(jnp.bfloat16), stats], axis=1)
    got = lax.all_to_all(send.reshape(n_plane, col, width + LANES), PLANE, 0, 0, tiled=True)
    tops = joined([got[:, :, width + k] for k in range(3)])
    totals = joined([got[:, :, width + k] for k in range(3, 6)])
    top1 = jnp.max(tops, axis=0)
    scale = jnp.exp(tops - top1[None])
    total1 = jnp.sum(scale * totals, axis=0)
    near1 = jnp.sum(scale[:, :, None] * got[:, :, :width].astype(jnp.float32), axis=0)

    flat = jnp.concatenate(pieces(top1) + pieces(total1))
    flat = jnp.pad(flat, (0, row_dev * LANES - flat.shape[0])).reshape(row_dev, LANES)
    send = jnp.concatenate(
        [
            near1.astype(jnp.bfloat16).reshape(n_z, row_dev, width),
            jnp.broadcast_to(flat[None], (n_z, row_dev, LANES)),
        ],
        axis=2,
    )
    got = lax.all_to_all(send, "z", 0, 0, tiled=True)
    flats = got[:, :, width:].reshape(n_z, row_dev * LANES)
    cut = [flats[:, k * col : (k + 1) * col] for k in range(6)]
    tops, totals = joined(cut[:3]), joined(cut[3:])
    top2 = jnp.max(tops, axis=0)
    lse_col = top2 + jnp.log(jnp.sum(jnp.exp(tops - top2[None]) * totals, axis=0))
    first = lax.axis_index("z") * row_dev
    own_lse = lax.dynamic_slice_in_dim(lse_col, first, row_dev, 0)
    own_tops = lax.dynamic_slice_in_dim(tops, first, row_dev, 1)
    scale = jnp.exp(own_tops - own_lse[None])
    targets = jnp.sum(scale[:, :, None] * got[:, :, :width].astype(jnp.float32), axis=0)

    lse = spread(lse_col[None], PLANE).reshape(-1)
    mass = lax.psum(jnp.sum(jnp.exp(score - lse[:, None]), axis=0), GRP)
    new_weights = weights + ETA * (1.0 - float(n_sites) / float(n_rows) * mass)
    noise_f = noise.astype(jnp.float32)
    potentials = jnp.sum(noise_f * noise_f, axis=1) / (2.0 * width) - EPS * (own_lse - math.log(float(n_sites)))
    return targets.astype(jnp.bfloat16), potentials, new_weights


def solution(mesh):
    fine = Mesh(np.asarray(mesh.devices).reshape(2, 2, 2, 16, 4), EVERY)
    in_specs = (P(EVERY, None), P(SITE, None), P(SITE))
    out_specs = (P(EVERY, None), P(EVERY), P(SITE))
    return jax.shard_map(shards, mesh=fine, in_specs=in_specs, out_specs=out_specs, check_vma=False)
```

```python
import math

import jax
import jax.numpy as jnp
import numpy as np
from jax import lax
from jax.sharding import Mesh
from jax.sharding import PartitionSpec as P

EPS = 0.006
ETA = 0.05
NEAR = ("x", "yl", "zl")
FAR = "zh"
SITE = ("yl", "zh", "zl", "x")
GRP = ("yh", "core")
EVERY = GRP + SITE
bf16, f32 = jnp.bfloat16, jnp.float32


def halves(v):
    hi = lax.reduce_precision(v, 8, 7)
    return hi.astype(bf16), lax.reduce_precision(v - hi, 8, 7).astype(bf16)


def joined(hi, low):
    return hi.astype(f32) + low.astype(f32)


def exchange(v, axes):
    return lax.all_to_all(v, axes, 0, 0, tiled=True)


def spread(v, axes):
    return exchange(jnp.broadcast_to(v[None], (lax.axis_size(axes),) + v.shape), axes)


def shards(noise, sites, weights):
    own, width = noise.shape
    n_near, n_far = lax.axis_size(NEAR), lax.axis_size(FAR)
    col = n_far * own
    n_rows = n_near * col
    all_sites = sites.shape[0] * lax.axis_size(SITE)
    all_rows = own * lax.axis_size(EVERY)
    sites_f = sites.astype(f32)
    half_sq = jnp.sum(sites_f * sites_f, axis=1) / (2.0 * width)
    rows = spread(spread(noise, FAR).reshape(col, width), NEAR).reshape(n_rows, width)
    inner = lax.dot_general(rows, sites, (((1,), (1,)), ((), ())), preferred_element_type=f32)
    score = weights[None, :] + (inner / width - half_sq[None, :]) / EPS
    top = halves(jnp.max(score, axis=1))
    part = jnp.exp(score - joined(*top)[:, None])
    total = halves(jnp.sum(part, axis=1))
    near = jnp.dot(part.astype(bf16), sites, preferred_element_type=f32).astype(bf16)

    stats = jnp.concatenate(top + total).reshape(col, -1)
    lanes = stats.shape[1]
    send = jnp.concatenate(
        [near.reshape(n_near, col, width), jnp.broadcast_to(stats[None], (n_near, col, lanes))], axis=2
    )
    got = exchange(send, NEAR)
    parts = got[:, :, width:].reshape(n_near, 4, n_rows)
    tops, totals = joined(parts[:, 0], parts[:, 1]), joined(parts[:, 2], parts[:, 3])
    top1 = jnp.max(tops, axis=0)
    scale = jnp.exp(tops - top1[None])
    total1 = jnp.sum(scale * totals, axis=0)
    first = (lax.axis_index(NEAR)) * col
    scale = lax.dynamic_slice_in_dim(scale, first, col, 1)
    near1 = jnp.sum(scale[:, :, None] * got[:, :, :width].astype(f32), axis=0).astype(bf16)

    stats = jnp.concatenate(halves(top1) + halves(total1)).reshape(own, -1)
    lanes = stats.shape[1]
    send = jnp.concatenate(
        [near1.reshape(n_far, own, width), jnp.broadcast_to(stats[None], (n_far, own, lanes))], axis=2
    )
    got = exchange(send, FAR)
    parts = got[:, :, width:].reshape(n_far, 4, n_rows)
    tops, totals = joined(parts[:, 0], parts[:, 1]), joined(parts[:, 2], parts[:, 3])
    top2 = jnp.max(tops, axis=0)
    lse = top2 + jnp.log(jnp.sum(jnp.exp(tops - top2[None]) * totals, axis=0))

    mass = jnp.sum(spread(jnp.sum(jnp.exp(score - lse[:, None]), axis=0)[None], GRP), axis=(0, 1))
    new_weights = weights + ETA * (1.0 - float(all_sites) / float(all_rows) * mass)

    first = first + lax.axis_index(FAR) * own
    own_lse = lax.dynamic_slice_in_dim(lse, first, own, 0)
    scale = jnp.exp(lax.dynamic_slice_in_dim(tops, first, own, 1) - own_lse[None])
    targets = jnp.sum(scale[:, :, None] * got[:, :, :width].astype(f32), axis=0)
    noise_f = noise.astype(f32)
    potentials = jnp.sum(noise_f * noise_f, axis=1) / (2.0 * width) - EPS * (own_lse - math.log(float(all_sites)))
    return targets.astype(bf16), potentials, new_weights


def solution(mesh):
    fine = Mesh(np.asarray(mesh.devices).reshape(2, 2, 2, 8, 2, 4), EVERY)
    in_specs = (P(EVERY, None), P(SITE, None), P(SITE))
    out_specs = (P(EVERY, None), P(EVERY), P(SITE))
    return jax.shard_map(shards, mesh=fine, in_specs=in_specs, out_specs=out_specs, check_vma=False)
```

```python
import functools
import math

import jax
import jax.numpy as jnp
import numpy as np
from jax import lax
from jax.experimental import pallas as pl
from jax.experimental.pallas import tpu as pltpu
from jax.sharding import Mesh
from jax.sharding import PartitionSpec as P

EPS = 0.006
ETA = 0.05
NEAR = ("x", "yl")
FAR = "z"
SITE = ("yl", "z", "x")
GRP = ("yh", "core")
EVERY = GRP + SITE
FINE = (2, 2, 2, 16, 4)
LANES = 128
bf16, f32 = jnp.bfloat16, jnp.float32
VMEM = pl.BlockSpec(memory_space=pltpu.VMEM)
PARAMS = pltpu.CompilerParams(vmem_limit_bytes=40 * 2**20)


def halves(v):
    hi = v.astype(bf16).astype(f32)
    return hi, (v - hi).astype(bf16).astype(f32)


def lane_of(shape):
    return lax.broadcasted_iota(jnp.int32, shape, len(shape) - 1)


def left(v, by):
    return jnp.roll(v, -by, axis=-1) if v.shape[-1] < LANES else pltpu.roll(v, LANES - by, v.ndim - 1)


def partial_targets(n_near, noise, sites, weights, half_sq, send, score_out):
    n_rows, width = noise.shape
    col = n_rows // n_near
    inner = lax.dot_general(noise[...], sites[...], (((1,), (1,)), ((), ())), preferred_element_type=f32)
    score = weights[...] + (inner / width - half_sq[...]) / EPS
    score_out[...] = score
    hi, low = halves(jnp.max(score, axis=1, keepdims=True))
    part = jnp.exp(score - (hi + low))
    stats = (hi, low) + halves(jnp.sum(part, axis=1, keepdims=True))
    lane = lane_of((col, LANES))
    tile = jnp.zeros((col, LANES), f32)
    for k in range(n_near):
        for p in range(4):
            tile = jnp.where(lane == 4 * k + p, stats[p][k * col : (k + 1) * col], tile)
    tile = tile.astype(bf16)
    for k in range(n_near):
        send[k * col : (k + 1) * col, width:] = tile
    send[:, :width] = jnp.dot(part.astype(bf16), sites[...], preferred_element_type=f32).astype(bf16)


def near_merge(n_near, own_k, got, out, stats):
    col, width = out.shape
    both = [got[s, :, width:].astype(f32) for s in range(n_near)]
    both = [v + left(v, 1) for v in both]
    first = lane_of((col, LANES)) % 4 == 0
    tops = [jnp.where(first, v, 0.0) for v in both]
    top = functools.reduce(jnp.maximum, tops)
    scales = [jnp.where(first, jnp.exp(v - top), 0.0) for v in tops]
    total = sum(c * jnp.where(first, left(v, 2), 0.0) for c, v in zip(scales, both))
    hi, low = halves(top)
    t_hi, t_low = halves(total)
    lane = lane_of((col, LANES)) % 4
    tile = jnp.where(lane == 0, hi, 0.0)
    for p, v in ((1, low), (2, t_hi), (3, t_low)):
        tile = jnp.where(lane == p, pltpu.roll(v, p, 1), tile)
    stats[...] = tile.astype(bf16)
    mine = lane_of((col, LANES)) == 4 * own_k[0]
    acc = jnp.zeros((col, width), f32)
    for s in range(n_near):
        c = jnp.sum(jnp.where(mine, scales[s], 0.0), axis=1, keepdims=True)
        acc = acc + c * got[s, :, :width].astype(f32)
    out[...] = acc.astype(bf16)


def normalise(n_near, got, score, mass, lse_out, scale_out):
    n_far, col, _ = got.shape
    first = lane_of((col, LANES)) % 4 == 0
    both = [got[s].astype(f32) for s in range(n_far)]
    both = [v + left(v, 1) for v in both]
    tops = [jnp.where(first, v, 0.0) for v in both]
    top = functools.reduce(jnp.maximum, tops)
    total = sum(jnp.where(first, jnp.exp(t - top) * left(v, 2), 1.0 / n_far) for t, v in zip(tops, both))
    lse = jnp.where(first, top + jnp.log(total), 0.0)
    lse_out[...] = lse
    for s in range(n_far):
        scale_out[s] = jnp.where(first, jnp.exp(tops[s] - lse), 0.0)
    lane = lane_of((col, LANES))
    acc = jnp.zeros((col, score.shape[1]), f32)
    for k in range(n_near):
        shift = jnp.sum(jnp.where(lane == 4 * k, lse, 0.0), axis=1, keepdims=True)
        acc = acc + jnp.exp(score[k * col : (k + 1) * col] - shift)
    mass[...] = jnp.sum(acc, axis=0, keepdims=True)


def run(kernel, outs, *args, first=None):
    specs = [VMEM] * len(args)
    if first is not None:
        args, specs = (first,) + args, [pl.BlockSpec(memory_space=pltpu.SMEM)] + specs
    return pl.pallas_call(
        kernel,
        out_shape=[jax.ShapeDtypeStruct(*o) for o in outs],
        in_specs=specs,
        out_specs=[VMEM] * len(outs),
        compiler_params=PARAMS,
    )(*args)


def exchange(v, axes):
    return lax.all_to_all(v, axes, 0, 0, tiled=True)


def spread(v, axes):
    return exchange(jnp.broadcast_to(v[None], (lax.axis_size(axes),) + v.shape), axes)


def shards(noise, sites, weights):
    own, width = noise.shape
    n_near, n_far = lax.axis_size(NEAR), lax.axis_size(FAR)
    col = n_far * own
    n_rows = n_near * col
    mine = sites.shape[0]
    all_sites = mine * lax.axis_size(SITE)
    all_rows = own * lax.axis_size(EVERY)
    sites_f = sites.astype(f32)
    half_sq = jnp.sum(sites_f * sites_f, axis=1) / (2.0 * width)
    rows = spread(spread(noise, FAR).reshape(col, width), NEAR).reshape(n_rows, width)
    send, score = run(
        functools.partial(partial_targets, n_near),
        [((n_rows, width + LANES), bf16), ((n_rows, mine), f32)],
        rows,
        sites,
        weights[None],
        half_sq[None],
    )

    got = exchange(send.reshape(n_near, col, width + LANES), NEAR)
    own_k = lax.axis_index(NEAR)
    part, stats = run(
        lambda k, *refs: near_merge(n_near, k, *refs),
        [((col, width), bf16), ((col, LANES), bf16)],
        got,
        first=own_k[None],
    )

    stats = stats[:, : 4 * n_near].reshape(own, -1)
    stats = jnp.broadcast_to(stats[None], (n_far,) + stats.shape)
    got = exchange(jnp.concatenate([part.reshape(n_far, own, width), stats], axis=2), FAR)
    stats = got[:, :, width:].reshape(n_far, col, 4 * n_near)
    stats = jnp.pad(stats, ((0, 0), (0, 0), (0, LANES - 4 * n_near)))
    mass, lse, scale = run(
        functools.partial(normalise, n_near),
        [((1, mine), f32), ((col, LANES), f32), ((n_far, col, LANES), f32)],
        stats,
        score,
    )
    mass = lax.psum(mass[0], GRP)
    new_weights = weights + ETA * (1.0 - float(all_sites) / float(all_rows) * mass)

    at = (lax.axis_index(FAR) * own, own_k * 4)
    own_lse = lax.dynamic_slice(lse, at, (own, 1))[:, 0]
    scale = lax.dynamic_slice(scale, (0,) + at, (n_far, own, 1))
    targets = jnp.sum(scale * got[:, :, :width].astype(f32), axis=0)
    noise_f = noise.astype(f32)
    potentials = jnp.sum(noise_f * noise_f, axis=1) / (2.0 * width) - EPS * (own_lse - math.log(float(all_sites)))
    return targets.astype(bf16), potentials, new_weights


def solution(mesh):
    fine = Mesh(np.asarray(mesh.devices).reshape(FINE), EVERY)
    in_specs = (P(EVERY, None), P(SITE, None), P(SITE))
    out_specs = (P(EVERY, None), P(EVERY), P(SITE))
    return jax.shard_map(shards, mesh=fine, in_specs=in_specs, out_specs=out_specs, check_vma=False)
```

```python
import functools
import math

import jax
import jax.numpy as jnp
import numpy as np
from jax import lax
from jax.experimental import pallas as pl
from jax.experimental.pallas import tpu as pltpu
from jax.sharding import Mesh
from jax.sharding import PartitionSpec as P

EPS = 0.006
ETA = 0.05
NEAR = ("x", "yl")
FAR = "z"
SITE = ("yl", "z", "x")
GRP = ("yh", "core")
EVERY = GRP + SITE
FINE = (2, 2, 2, 16, 4)
LANES = 128
bf16, f32 = jnp.bfloat16, jnp.float32
VMEM = pl.BlockSpec(memory_space=pltpu.VMEM)
PARAMS = pltpu.CompilerParams(vmem_limit_bytes=40 * 2**20)


def halves(v):
    hi = v.astype(bf16).astype(f32)
    return hi, (v - hi).astype(bf16).astype(f32)


def lane_of(shape):
    return lax.broadcasted_iota(jnp.int32, shape, len(shape) - 1)


def left(v, by):
    return jnp.roll(v, -by, axis=-1) if v.shape[-1] < LANES else pltpu.roll(v, LANES - by, v.ndim - 1)


def partial_targets(n_near, noise, sites, weights, send, score_out):
    n_rows, width = noise.shape
    col = n_rows // n_near
    squares = jnp.zeros((sites.shape[0], LANES), f32)
    for c in range(0, width, LANES):
        part = sites[:, c : c + LANES].astype(f32)
        squares = squares + part * part
    half_sq = jnp.sum(squares.T, axis=0, keepdims=True) / (2.0 * width)
    inner = lax.dot_general(noise[...], sites[...], (((1,), (1,)), ((), ())), preferred_element_type=f32)
    score = weights[...] + (inner / width - half_sq) / EPS
    score_out[...] = score
    hi, low = halves(jnp.max(score, axis=1, keepdims=True))
    part = jnp.exp(score - (hi + low))
    stats = (hi, low) + halves(jnp.sum(part, axis=1, keepdims=True))
    lane = lane_of((col, LANES))
    tile = jnp.zeros((col, LANES), f32)
    for k in range(n_near):
        for p in range(4):
            tile = jnp.where(lane == 4 * k + p, stats[p][k * col : (k + 1) * col], tile)
    tile = tile.astype(bf16)
    for k in range(n_near):
        send[k * col : (k + 1) * col, width:] = tile
    send[:, :width] = jnp.dot(part.astype(bf16), sites[...], preferred_element_type=f32).astype(bf16)


def near_merge(n_near, own_k, got, out, stats):
    col, width = out.shape
    both = [got[s, :, width:].astype(f32) for s in range(n_near)]
    both = [v + left(v, 1) for v in both]
    first = lane_of((col, LANES)) % 4 == 0
    tops = [jnp.where(first, v, 0.0) for v in both]
    top = functools.reduce(jnp.maximum, tops)
    scales = [jnp.where(first, jnp.exp(v - top), 0.0) for v in tops]
    total = sum(c * jnp.where(first, left(v, 2), 0.0) for c, v in zip(scales, both))
    hi, low = halves(top)
    t_hi, t_low = halves(total)
    lane = lane_of((col, LANES)) % 4
    tile = jnp.where(lane == 0, hi, 0.0)
    for p, v in ((1, low), (2, t_hi), (3, t_low)):
        tile = jnp.where(lane == p, pltpu.roll(v, p, 1), tile)
    stats[...] = tile.astype(bf16)
    mine = lane_of((col, LANES)) == 4 * own_k[0]
    acc = jnp.zeros((col, width), f32)
    for s in range(n_near):
        c = jnp.sum(jnp.where(mine, scales[s], 0.0), axis=1, keepdims=True)
        acc = acc + c * got[s, :, :width].astype(f32)
    out[...] = acc.astype(bf16)


def normalise(n_near, got, score, mass, lse_out, scale_out):
    n_far, col, _ = got.shape
    first = lane_of((col, LANES)) % 4 == 0
    both = [got[s].astype(f32) for s in range(n_far)]
    both = [v + left(v, 1) for v in both]
    tops = [jnp.where(first, v, 0.0) for v in both]
    top = functools.reduce(jnp.maximum, tops)
    total = sum(jnp.where(first, jnp.exp(t - top) * left(v, 2), 1.0 / n_far) for t, v in zip(tops, both))
    lse = jnp.where(first, top + jnp.log(total), 0.0)
    lse_out[...] = lse
    for s in range(n_far):
        scale_out[s] = jnp.where(first, jnp.exp(tops[s] - lse), 0.0)
    lane = lane_of((col, LANES))
    acc = jnp.zeros((col, score.shape[1]), f32)
    for k in range(n_near):
        shift = jnp.sum(jnp.where(lane == 4 * k, lse, 0.0), axis=1, keepdims=True)
        acc = acc + jnp.exp(score[k * col : (k + 1) * col] - shift)
    mass[...] = jnp.sum(acc, axis=0, keepdims=True)


def run(kernel, outs, *args, first=None):
    specs = [VMEM] * len(args)
    if first is not None:
        args, specs = (first,) + args, [pl.BlockSpec(memory_space=pltpu.SMEM)] + specs
    return pl.pallas_call(
        kernel,
        out_shape=[jax.ShapeDtypeStruct(*o) for o in outs],
        in_specs=specs,
        out_specs=[VMEM] * len(outs),
        compiler_params=PARAMS,
    )(*args)


def exchange(v, axes):
    return lax.all_to_all(v, axes, 0, 0, tiled=True)


def spread(v, axes):
    return exchange(jnp.broadcast_to(v[None], (lax.axis_size(axes),) + v.shape), axes)


def shards(noise, sites, weights):
    own, width = noise.shape
    n_near, n_far = lax.axis_size(NEAR), lax.axis_size(FAR)
    col = n_far * own
    n_rows = n_near * col
    mine = sites.shape[0]
    all_sites = mine * lax.axis_size(SITE)
    all_rows = own * lax.axis_size(EVERY)
    noise_f = noise.astype(f32)
    noise_sq = jnp.sum(noise_f * noise_f, axis=1) / (2.0 * width)
    own_k = lax.axis_index(NEAR)
    at = ((lax.axis_index(FAR) * own).astype(jnp.uint32), (own_k * 4).astype(jnp.uint32))
    noise, noise_sq, own_k, at = lax.optimization_barrier((noise, noise_sq, own_k, at))
    rows = spread(spread(noise, FAR).reshape(col, width), NEAR).reshape(n_rows, width)
    send, score = run(
        functools.partial(partial_targets, n_near),
        [((n_rows, width + LANES), bf16), ((n_rows, mine), f32)],
        rows,
        sites,
        weights[None],
    )

    got = exchange(send.reshape(n_near, col, width + LANES), NEAR)
    part, stats = run(
        lambda k, *refs: near_merge(n_near, k, *refs),
        [((col, width), bf16), ((col, LANES), bf16)],
        got,
        first=own_k[None],
    )

    stats = stats[:, : 4 * n_near].reshape(own, -1)
    stats = jnp.broadcast_to(stats[None], (n_far,) + stats.shape)
    got = exchange(jnp.concatenate([part.reshape(n_far, own, width), stats], axis=2), FAR)
    stats = got[:, :, width:].reshape(n_far, col, 4 * n_near)
    stats = jnp.pad(stats, ((0, 0), (0, 0), (0, LANES - 4 * n_near)))
    mass, lse, scale = run(
        functools.partial(normalise, n_near),
        [((1, mine), f32), ((col, LANES), f32), ((n_far, col, LANES), f32)],
        stats,
        score,
    )
    mass = lax.psum(mass[0], GRP)
    new_weights = weights + ETA * (1.0 - float(all_sites) / float(all_rows) * mass)

    own_lse = lax.dynamic_slice(lse, at, (own, 1))[:, 0]
    scale = lax.dynamic_slice(scale, (jnp.uint32(0),) + at, (n_far, own, 1))
    targets = jnp.sum(scale * got[:, :, :width].astype(f32), axis=0)
    potentials = noise_sq - EPS * (own_lse - math.log(float(all_sites)))
    return targets.astype(bf16), potentials, new_weights


def solution(mesh):
    fine = Mesh(np.asarray(mesh.devices).reshape(FINE), EVERY)
    in_specs = (P(EVERY, None), P(SITE, None), P(SITE))
    out_specs = (P(EVERY, None), P(EVERY), P(SITE))
    return jax.shard_map(shards, mesh=fine, in_specs=in_specs, out_specs=out_specs, check_vma=False)
```

```python
import functools
import math

import jax
import jax.numpy as jnp
import numpy as np
from jax import lax
from jax.experimental import pallas as pl
from jax.experimental.pallas import tpu as pltpu
from jax.sharding import Mesh
from jax.sharding import PartitionSpec as P

EPS = 0.006
ETA = 0.05
NEAR = ("x", "yl", "zl")
FAR = "zh"
SITE = ("yl", "zh", "zl", "x")
GRP = ("yh", "core")
EVERY = GRP + SITE
FINE = (2, 2, 2, 8, 2, 4)
LANES = 128
bf16, f32 = jnp.bfloat16, jnp.float32
VMEM = pl.BlockSpec(memory_space=pltpu.VMEM)
PARAMS = pltpu.CompilerParams(vmem_limit_bytes=40 * 2**20)


def halves(v):
    hi = v.astype(bf16).astype(f32)
    return hi, (v - hi).astype(bf16).astype(f32)


def lane_of(shape):
    return lax.broadcasted_iota(jnp.int32, shape, len(shape) - 1)


def left(v, by):
    return jnp.roll(v, -by, axis=-1) if v.shape[-1] < LANES else pltpu.roll(v, LANES - by, v.ndim - 1)


def partial_targets(n_near, noise, sites, weights, send, score_out):
    n_rows, width = noise.shape
    col = n_rows // n_near
    squares = jnp.zeros((sites.shape[0], LANES), f32)
    for c in range(0, width, LANES):
        part = sites[:, c : c + LANES].astype(f32)
        squares = squares + part * part
    half_sq = jnp.sum(squares.T, axis=0, keepdims=True) / (2.0 * width)
    inner = lax.dot_general(noise[...], sites[...], (((1,), (1,)), ((), ())), preferred_element_type=f32)
    score = weights[...] + (inner / width - half_sq) / EPS
    score_out[...] = score
    hi, low = halves(jnp.max(score, axis=1, keepdims=True))
    part = jnp.exp(score - (hi + low))
    stats = (hi, low) + halves(jnp.sum(part, axis=1, keepdims=True))
    lane = lane_of((col, LANES))
    tile = jnp.zeros((col, LANES), f32)
    for k in range(n_near):
        for p in range(4):
            tile = jnp.where(lane == 4 * k + p, stats[p][k * col : (k + 1) * col], tile)
    tile = tile.astype(bf16)
    for k in range(n_near):
        send[k * col : (k + 1) * col, width:] = tile
    send[:, :width] = jnp.dot(part.astype(bf16), sites[...], preferred_element_type=f32).astype(bf16)


def near_merge(n_near, own_k, got, out, stats):
    col, width = out.shape
    both = [got[s, :, width:].astype(f32) for s in range(n_near)]
    both = [v + left(v, 1) for v in both]
    first = lane_of((col, LANES)) % 4 == 0
    tops = [jnp.where(first, v, 0.0) for v in both]
    top = functools.reduce(jnp.maximum, tops)
    scales = [jnp.where(first, jnp.exp(v - top), 0.0) for v in tops]
    total = sum(c * jnp.where(first, left(v, 2), 0.0) for c, v in zip(scales, both))
    hi, low = halves(top)
    t_hi, t_low = halves(total)
    lane = lane_of((col, LANES)) % 4
    tile = jnp.where(lane == 0, hi, 0.0)
    for p, v in ((1, low), (2, t_hi), (3, t_low)):
        tile = jnp.where(lane == p, pltpu.roll(v, p, 1), tile)
    stats[...] = tile.astype(bf16)
    mine = lane_of((col, LANES)) == 4 * own_k[0]
    acc = jnp.zeros((col, width), f32)
    for s in range(n_near):
        c = jnp.sum(jnp.where(mine, scales[s], 0.0), axis=1, keepdims=True)
        acc = acc + c * got[s, :, :width].astype(f32)
    out[...] = acc.astype(bf16)


def normalise(n_near, all_sites, at, stats, got, score, noise, mass, targets, potentials):
    n_far, col, _ = stats.shape
    own, width = noise.shape
    lane = lane_of((col, LANES))
    first = lane % 4 == 0
    both = [stats[s].astype(f32) for s in range(n_far)]
    both = [v + left(v, 1) for v in both]
    tops = [jnp.where(first, v, 0.0) for v in both]
    top = functools.reduce(jnp.maximum, tops)
    total = sum(jnp.where(first, jnp.exp(t - top) * left(v, 2), 1.0 / n_far) for t, v in zip(tops, both))
    lse = jnp.where(first, top + jnp.log(total), 0.0)
    acc = jnp.zeros((col, score.shape[1]), f32)
    for k in range(n_near):
        shift = jnp.sum(jnp.where(lane == 4 * k, lse, 0.0), axis=1, keepdims=True)
        acc = acc + jnp.exp(score[k * col : (k + 1) * col] - shift)
    mass[...] = jnp.sum(acc, axis=0, keepdims=True)

    sub = lax.broadcasted_iota(jnp.int32, (col, LANES), 0)
    here = [(sub == at[0] + r) & (lane == at[1]) for r in range(own)]
    row = lax.broadcasted_iota(jnp.int32, (own, 1), 0)

    def owned(v):
        picked = jnp.zeros((own, 1), f32)
        for r in range(own):
            value = jnp.sum(jnp.where(here[r], v, 0.0), axis=(0, 1), keepdims=True)
            picked = jnp.where(row == r, value, picked)
        return picked

    own_lse = owned(lse)
    total = jnp.zeros((own, width), f32)
    for s in range(n_far):
        total = total + jnp.exp(owned(tops[s]) - own_lse) * got[s, :, :width].astype(f32)
    targets[...] = total.astype(bf16)
    squares = noise[...].astype(f32)
    squares = jnp.sum(squares * squares, axis=1, keepdims=True)
    potentials[...] = squares / (2.0 * width) - EPS * (own_lse - math.log(float(all_sites)))


def run(kernel, outs, *args, first=None):
    specs = [VMEM] * len(args)
    if first is not None:
        args, specs = (first,) + args, [pl.BlockSpec(memory_space=pltpu.SMEM)] + specs
    return pl.pallas_call(
        kernel,
        out_shape=[jax.ShapeDtypeStruct(*o) for o in outs],
        in_specs=specs,
        out_specs=[VMEM] * len(outs),
        compiler_params=PARAMS,
    )(*args)


def exchange(v, axes):
    return lax.all_to_all(v, axes, 0, 0, tiled=True)


def spread(v, axes):
    return exchange(jnp.broadcast_to(v[None], (lax.axis_size(axes),) + v.shape), axes)


def gather_rows(noise):
    own, width = noise.shape
    rows = lax.all_gather(noise, ("zh", "zl"), axis=0)
    rows = rows.reshape(lax.axis_size("zh"), lax.axis_size("zl"), own, width)
    rows = jnp.transpose(rows, (1, 0, 2, 3)).reshape(-1, width)
    return spread(rows, ("x", "yl")).reshape(-1, width)


def shards(noise, sites, weights):
    own, width = noise.shape
    n_near, n_far = lax.axis_size(NEAR), lax.axis_size(FAR)
    col = n_far * own
    n_rows = n_near * col
    mine = sites.shape[0]
    all_sites = mine * lax.axis_size(SITE)
    all_rows = own * lax.axis_size(EVERY)
    own_k = lax.axis_index(NEAR)
    at = jnp.stack([lax.axis_index(FAR) * own, own_k * 4])
    noise, own_k, at = lax.optimization_barrier((noise, own_k, at))
    rows = gather_rows(noise)
    send, score = run(
        functools.partial(partial_targets, n_near),
        [((n_rows, width + LANES), bf16), ((n_rows, mine), f32)],
        rows,
        sites,
        weights[None],
    )

    got = exchange(send.reshape(n_near, col, width + LANES), NEAR)
    part, stats = run(
        lambda k, *refs: near_merge(n_near, k, *refs),
        [((col, width), bf16), ((col, LANES), bf16)],
        got,
        first=own_k[None],
    )

    stats = stats[:, : 4 * n_near].reshape(own, -1)
    stats = jnp.broadcast_to(stats[None], (n_far,) + stats.shape)
    got = exchange(jnp.concatenate([part.reshape(n_far, own, width), stats], axis=2), FAR)
    stats = got[:, :, width:].reshape(n_far, col, 4 * n_near)
    stats = jnp.pad(stats, ((0, 0), (0, 0), (0, LANES - 4 * n_near)))
    mass, targets, potentials = run(
        lambda at, *refs: normalise(n_near, all_sites, at, *refs),
        [((1, mine), f32), ((own, width), bf16), ((own, 1), f32)],
        stats,
        got,
        score,
        noise,
        first=at,
    )
    mass = lax.psum(mass[0], GRP)
    new_weights = weights + ETA * (1.0 - float(all_sites) / float(all_rows) * mass)
    return targets, potentials[:, 0], new_weights


def solution(mesh):
    fine = Mesh(np.asarray(mesh.devices).reshape(FINE), EVERY)
    in_specs = (P(EVERY, None), P(SITE, None), P(SITE))
    out_specs = (P(EVERY, None), P(EVERY), P(SITE))
    return jax.shard_map(shards, mesh=fine, in_specs=in_specs, out_specs=out_specs, check_vma=False)
```

```python
import functools
import math

import jax
import jax.numpy as jnp
import numpy as np
from jax import lax
from jax.experimental import pallas as pl
from jax.experimental.pallas import tpu as pltpu
from jax.sharding import Mesh
from jax.sharding import PartitionSpec as P

EPS = 0.006
ETA = 0.05
NEAR = ("x", "yl", "zl")
FAR = "zh"
SITE = ("yl", "zh", "zl", "x")
GRP = ("yh", "core")
EVERY = GRP + SITE
FINE = (2, 2, 2, 8, 2, 4)
LANES = 128
bf16, f32 = jnp.bfloat16, jnp.float32
VMEM = pl.BlockSpec(memory_space=pltpu.VMEM)
PARAMS = pltpu.CompilerParams(vmem_limit_bytes=40 * 2**20)


def halves(v):
    hi = v.astype(bf16).astype(f32)
    return hi, (v - hi).astype(bf16).astype(f32)


def lane_of(shape):
    return lax.broadcasted_iota(jnp.int32, shape, len(shape) - 1)


def left(v, by):
    return jnp.roll(v, -by, axis=-1) if v.shape[-1] < LANES else pltpu.roll(v, LANES - by, v.ndim - 1)


def partial_targets(n_near, noise, sites, weights, send, score_out):
    n_rows, width = noise.shape
    col = n_rows // n_near
    squares = jnp.zeros((sites.shape[0], LANES), f32)
    for c in range(0, width, LANES):
        part = sites[:, c : c + LANES].astype(f32)
        squares = squares + part * part
    half_sq = jnp.sum(squares.T, axis=0, keepdims=True) / (2.0 * width)
    inner = lax.dot_general(noise[...], sites[...], (((1,), (1,)), ((), ())), preferred_element_type=f32)
    score = weights[...] + (inner / width - half_sq) / EPS
    score_out[...] = score
    hi, low = halves(jnp.max(score, axis=1, keepdims=True))
    part = jnp.exp(score - (hi + low))
    stats = (hi, low) + halves(jnp.sum(part, axis=1, keepdims=True))
    lane = lane_of((col, LANES))
    tile = jnp.zeros((col, LANES), f32)
    for k in range(n_near):
        for p in range(4):
            tile = jnp.where(lane == 4 * k + p, stats[p][k * col : (k + 1) * col], tile)
    tile = tile.astype(bf16)
    for k in range(n_near):
        send[k * col : (k + 1) * col, width:] = tile
    send[:, :width] = jnp.dot(part.astype(bf16), sites[...], preferred_element_type=f32).astype(bf16)


def near_merge(n_near, own_k, got, out, stats):
    col, width = out.shape
    both = [got[s, :, width:].astype(f32) for s in range(n_near)]
    both = [v + left(v, 1) for v in both]
    first = lane_of((col, LANES)) % 4 == 0
    tops = [jnp.where(first, v, 0.0) for v in both]
    top = functools.reduce(jnp.maximum, tops)
    scales = [jnp.where(first, jnp.exp(v - top), 0.0) for v in tops]
    total = sum(c * jnp.where(first, left(v, 2), 0.0) for c, v in zip(scales, both))
    hi, low = halves(top)
    t_hi, t_low = halves(total)
    lane = lane_of((col, LANES)) % 4
    tile = jnp.where(lane == 0, hi, 0.0)
    for p, v in ((1, low), (2, t_hi), (3, t_low)):
        tile = jnp.where(lane == p, pltpu.roll(v, p, 1), tile)
    stats[...] = tile.astype(bf16)
    mine = lane_of((col, LANES)) == 4 * own_k[0]
    acc = jnp.zeros((col, width), f32)
    for s in range(n_near):
        c = jnp.sum(jnp.where(mine, scales[s], 0.0), axis=1, keepdims=True)
        acc = acc + c * got[s, :, :width].astype(f32)
    out[...] = acc.astype(bf16)


def normalise(n_near, all_sites, gain, at, stats, got, score, noise, weights, change, targets, potentials):
    n_far, col, _ = stats.shape
    own, width = noise.shape
    lane = lane_of((col, LANES))
    first = lane % 4 == 0
    both = [stats[s].astype(f32) for s in range(n_far)]
    both = [v + left(v, 1) for v in both]
    tops = [jnp.where(first, v, 0.0) for v in both]
    top = functools.reduce(jnp.maximum, tops)
    total = sum(jnp.where(first, jnp.exp(t - top) * left(v, 2), 1.0 / n_far) for t, v in zip(tops, both))
    lse = jnp.where(first, top + jnp.log(total), 0.0)
    acc = jnp.zeros((col, score.shape[1]), f32)
    for k in range(n_near):
        shift = jnp.sum(jnp.where(lane == 4 * k, lse, 0.0), axis=1, keepdims=True)
        acc = acc + jnp.exp(score[k * col : (k + 1) * col] - shift)
    change[...] = jnp.where(at[2] == 0, weights[...] + ETA, 0.0) - gain * jnp.sum(acc, axis=0, keepdims=True)

    sub = lax.broadcasted_iota(jnp.int32, (col, LANES), 0)
    here = [(sub == at[0] + r) & (lane == at[1]) for r in range(own)]
    row = lax.broadcasted_iota(jnp.int32, (own, 1), 0)

    def owned(v):
        picked = jnp.zeros((own, 1), f32)
        for r in range(own):
            value = jnp.sum(jnp.where(here[r], v, 0.0), axis=(0, 1), keepdims=True)
            picked = jnp.where(row == r, value, picked)
        return picked

    own_lse = owned(lse)
    total = jnp.zeros((own, width), f32)
    for s in range(n_far):
        total = total + jnp.exp(owned(tops[s]) - own_lse) * got[s, :, :width].astype(f32)
    targets[...] = total.astype(bf16)
    squares = noise[...].astype(f32)
    squares = jnp.sum(squares * squares, axis=1, keepdims=True)
    value = squares / (2.0 * width) - EPS * (own_lse - math.log(float(all_sites)))
    flat = jnp.zeros((1, LANES), f32)
    for r in range(own):
        flat = jnp.where(lane_of((1, LANES)) == r, value[r : r + 1], flat)
    potentials[...] = flat[:, :own]


def run(kernel, outs, *args, first=None):
    specs = [VMEM] * len(args)
    if first is not None:
        args, specs = (first,) + args, [pl.BlockSpec(memory_space=pltpu.SMEM)] + specs
    return pl.pallas_call(
        kernel,
        out_shape=[jax.ShapeDtypeStruct(*o) for o in outs],
        in_specs=specs,
        out_specs=[VMEM] * len(outs),
        compiler_params=PARAMS,
    )(*args)


def exchange(v, axes):
    return lax.all_to_all(v, axes, 0, 0, tiled=True)


def spread(v, axes):
    return exchange(jnp.broadcast_to(v[None], (lax.axis_size(axes),) + v.shape), axes)


def gather_rows(noise):
    own, width = noise.shape
    rows = lax.all_gather(noise, ("zh", "zl"), axis=0)
    rows = rows.reshape(lax.axis_size("zh"), lax.axis_size("zl"), own, width)
    rows = jnp.transpose(rows, (1, 0, 2, 3)).reshape(-1, width)
    return spread(rows, ("x", "yl")).reshape(-1, width)


def shards(noise, sites, weights):
    own, width = noise.shape
    n_near, n_far = lax.axis_size(NEAR), lax.axis_size(FAR)
    col = n_far * own
    n_rows = n_near * col
    mine = sites.shape[0]
    all_sites = mine * lax.axis_size(SITE)
    all_rows = own * lax.axis_size(EVERY)
    own_k = lax.axis_index(NEAR)
    at = jnp.stack([lax.axis_index(FAR) * own, own_k * 4, lax.axis_index(GRP)])
    noise, own_k, at = lax.optimization_barrier((noise, own_k, at))
    rows = gather_rows(noise)
    send, score = run(
        functools.partial(partial_targets, n_near),
        [((n_rows, width + LANES), bf16), ((n_rows, mine), f32)],
        rows,
        sites,
        weights[None],
    )

    got = exchange(send.reshape(n_near, col, width + LANES), NEAR)
    part, stats = run(
        lambda k, *refs: near_merge(n_near, k, *refs),
        [((col, width), bf16), ((col, LANES), bf16)],
        got,
        first=own_k[None],
    )

    stats = stats[:, : 4 * n_near].reshape(own, -1)
    stats = jnp.broadcast_to(stats[None], (n_far,) + stats.shape)
    got = exchange(jnp.concatenate([part.reshape(n_far, own, width), stats], axis=2), FAR)
    stats = got[:, :, width:].reshape(n_far, col, 4 * n_near)
    stats = jnp.pad(stats, ((0, 0), (0, 0), (0, LANES - 4 * n_near)))
    gain = ETA * float(all_sites) / float(all_rows)
    change, targets, potentials = run(
        lambda at, *refs: normalise(n_near, all_sites, gain, at, *refs),
        [((1, mine), f32), ((own, width), bf16), ((1, own), f32)],
        stats,
        got,
        score,
        noise,
        weights[None],
        first=at,
    )
    return targets, potentials[0], lax.psum(change[0], GRP)


def solution(mesh):
    fine = Mesh(np.asarray(mesh.devices).reshape(FINE), EVERY)
    in_specs = (P(EVERY, None), P(SITE, None), P(SITE))
    out_specs = (P(EVERY, None), P(EVERY), P(SITE))
    return jax.shard_map(shards, mesh=fine, in_specs=in_specs, out_specs=out_specs, check_vma=False)
```

```python
import functools
import math

import jax
import jax.numpy as jnp
import numpy as np
from jax import lax
from jax.experimental import pallas as pl
from jax.experimental.pallas import tpu as pltpu
from jax.sharding import Mesh
from jax.sharding import PartitionSpec as P

EPS = 0.006
ETA = 0.05
NEAR = ("x", "yl", "zl")
FAR = "zh"
SITE = ("yl", "zh", "zl", "x")
GRP = ("yh", "core")
EVERY = GRP + SITE
FINE = (2, 2, 2, 8, 2, 4)
LANES = 128
bf16, f32 = jnp.bfloat16, jnp.float32
VMEM = pl.BlockSpec(memory_space=pltpu.VMEM)
PARAMS = pltpu.CompilerParams(vmem_limit_bytes=40 * 2**20)


def halves(v):
    hi = v.astype(bf16).astype(f32)
    return hi, (v - hi).astype(bf16).astype(f32)


def lane_of(shape):
    return lax.broadcasted_iota(jnp.int32, shape, len(shape) - 1)


def left(v, by):
    return jnp.roll(v, -by, axis=-1) if v.shape[-1] < LANES else pltpu.roll(v, LANES - by, v.ndim - 1)


def partial_targets(n_near, noise, sites, weights, send, score_out):
    n_rows, width = noise.shape
    col = n_rows // n_near
    squares = jnp.zeros((sites.shape[0], LANES), f32)
    for c in range(0, width, LANES):
        part = sites[:, c : c + LANES].astype(f32)
        squares = squares + part * part
    half_sq = jnp.sum(squares.T, axis=0, keepdims=True) / (2.0 * width)
    inner = lax.dot_general(noise[...], sites[...], (((1,), (1,)), ((), ())), preferred_element_type=f32)
    score = weights[...] + (inner / width - half_sq) / EPS
    score_out[...] = score
    hi, low = halves(jnp.max(score, axis=1, keepdims=True))
    part = jnp.exp(score - (hi + low))
    stats = (hi, low) + halves(jnp.sum(part, axis=1, keepdims=True))
    lane = lane_of((col, LANES))
    tile = jnp.zeros((col, LANES), f32)
    for k in range(n_near):
        for p in range(4):
            tile = jnp.where(lane == 4 * k + p, stats[p][k * col : (k + 1) * col], tile)
    tile = tile.astype(bf16)
    for k in range(n_near):
        send[k * col : (k + 1) * col, width:] = tile
    send[:, :width] = jnp.dot(part.astype(bf16), sites[...], preferred_element_type=f32).astype(bf16)


def near_merge(n_near, own_k, got, out, stats):
    col, width = out.shape
    both = [got[s, :, width:].astype(f32) for s in range(n_near)]
    both = [v + left(v, 1) for v in both]
    first = lane_of((col, LANES)) % 4 == 0
    tops = [jnp.where(first, v, 0.0) for v in both]
    top = functools.reduce(jnp.maximum, tops)
    scales = [jnp.where(first, jnp.exp(v - top), 0.0) for v in tops]
    total = sum(c * jnp.where(first, left(v, 2), 0.0) for c, v in zip(scales, both))
    hi, low = halves(top)
    t_hi, t_low = halves(total)
    lane = lane_of((col, LANES)) % 4
    tile = jnp.where(lane == 0, hi, 0.0)
    for p, v in ((1, low), (2, t_hi), (3, t_low)):
        tile = jnp.where(lane == p, pltpu.roll(v, p, 1), tile)
    stats[...] = tile.astype(bf16)
    mine = lane_of((col, LANES)) == 4 * own_k[0]
    acc = jnp.zeros((col, width), f32)
    for s in range(n_near):
        c = jnp.sum(jnp.where(mine, scales[s], 0.0), axis=1, keepdims=True)
        acc = acc + c * got[s, :, :width].astype(f32)
    out[...] = acc.astype(bf16)


def normalise(n_near, all_sites, gain, at, stats, got, score, noise, weights, change, targets, potentials):
    n_far, col, _ = stats.shape
    own, width = noise.shape
    lane = lane_of((col, LANES))
    first = lane % 4 == 0
    both = [stats[s].astype(f32) for s in range(n_far)]
    both = [v + left(v, 1) for v in both]
    tops = [jnp.where(first, v, 0.0) for v in both]
    top = functools.reduce(jnp.maximum, tops)
    total = sum(jnp.where(first, jnp.exp(t - top) * left(v, 2), 1.0 / n_far) for t, v in zip(tops, both))
    lse = jnp.where(first, top + jnp.log(total), 0.0)
    acc = jnp.zeros((col, score.shape[1]), f32)
    for k in range(n_near):
        shift = jnp.sum(jnp.where(lane == 4 * k, lse, 0.0), axis=1, keepdims=True)
        acc = acc + jnp.exp(score[k * col : (k + 1) * col] - shift)
    change[...] = jnp.where(at[2] == 0, weights[...] + ETA, 0.0) - gain * jnp.sum(acc, axis=0, keepdims=True)

    sub = lax.broadcasted_iota(jnp.int32, (col, LANES), 0)
    here = [(sub == at[0] + r) & (lane == at[1]) for r in range(own)]
    row = lax.broadcasted_iota(jnp.int32, (own, 1), 0)

    def owned(v):
        picked = jnp.zeros((own, 1), f32)
        for r in range(own):
            value = jnp.sum(jnp.where(here[r], v, 0.0), axis=(0, 1), keepdims=True)
            picked = jnp.where(row == r, value, picked)
        return picked

    own_lse = owned(lse)
    total = jnp.zeros((own, width), f32)
    for s in range(n_far):
        total = total + jnp.exp(owned(tops[s]) - own_lse) * got[s, :, :width].astype(f32)
    targets[...] = total.astype(bf16)
    squares = noise[...].astype(f32)
    squares = jnp.sum(squares * squares, axis=1, keepdims=True)
    value = squares / (2.0 * width) - EPS * (own_lse - math.log(float(all_sites)))
    flat = jnp.zeros((1, LANES), f32)
    for r in range(own):
        flat = jnp.where(lane_of((1, LANES)) == r, value[r : r + 1], flat)
    potentials[...] = flat[:, :own]


def run(kernel, outs, *args, first=None):
    specs = [VMEM] * len(args)
    if first is not None:
        args, specs = (first,) + args, [pl.BlockSpec(memory_space=pltpu.SMEM)] + specs
    return pl.pallas_call(
        kernel,
        out_shape=[jax.ShapeDtypeStruct(*o) for o in outs],
        in_specs=specs,
        out_specs=[VMEM] * len(outs),
        compiler_params=PARAMS,
    )(*args)


def exchange(v, axes):
    return lax.all_to_all(v, axes, 0, 0, tiled=True)


def spread(v, axes):
    return exchange(jnp.broadcast_to(v[None], (lax.axis_size(axes),) + v.shape), axes)


def gather_rows(noise):
    own, width = noise.shape
    rows = lax.all_gather(noise, ("zh", "zl"), axis=0)
    rows = rows.reshape(lax.axis_size("zh"), lax.axis_size("zl"), own, width)
    rows = jnp.transpose(rows, (1, 0, 2, 3)).reshape(-1, width)
    return spread(rows, ("x", "yl")).reshape(-1, width)


def shards(noise, sites, weights):
    own, width = noise.shape
    n_near, n_far = lax.axis_size(NEAR), lax.axis_size(FAR)
    col = n_far * own
    n_rows = n_near * col
    mine = sites.shape[0]
    all_sites = mine * lax.axis_size(SITE)
    all_rows = own * lax.axis_size(EVERY)
    own_k = lax.axis_index(NEAR)
    at = jnp.stack([lax.axis_index(FAR) * own, own_k * 4, lax.axis_index(GRP)])
    noise, own_k, at = lax.optimization_barrier((noise, own_k, at))
    rows = gather_rows(noise)
    send, score = run(
        functools.partial(partial_targets, n_near),
        [((n_rows, width + LANES), bf16), ((n_rows, mine), f32)],
        rows,
        sites,
        weights[None],
    )

    got = exchange(send.reshape(n_near, col, width + LANES), NEAR)
    part, stats = run(
        lambda k, *refs: near_merge(n_near, k, *refs),
        [((col, width), bf16), ((col, LANES), bf16)],
        got,
        first=own_k[None],
    )

    stats = stats[:, : 4 * n_near].reshape(own, -1)
    stats = jnp.broadcast_to(stats[None], (n_far,) + stats.shape)
    got = exchange(jnp.concatenate([part.reshape(n_far, own, width), stats], axis=2), FAR)
    stats = got[:, :, width:].reshape(n_far, col, 4 * n_near)
    stats = jnp.pad(stats, ((0, 0), (0, 0), (0, LANES - 4 * n_near)))
    gain = ETA * float(all_sites) / float(all_rows)
    change, targets, potentials = run(
        lambda at, *refs: normalise(n_near, all_sites, gain, at, *refs),
        [((1, mine), f32), ((own, width), bf16), ((1, own), f32)],
        stats,
        got,
        score,
        noise,
        weights[None],
        first=at,
    )
    return targets, potentials[0], lax.psum(change[0], ("core", "yh"))


def solution(mesh):
    fine = Mesh(np.asarray(mesh.devices).reshape(FINE), EVERY)
    in_specs = (P(EVERY, None), P(SITE, None), P(SITE))
    out_specs = (P(EVERY, None), P(EVERY), P(SITE))
    return jax.shard_map(shards, mesh=fine, in_specs=in_specs, out_specs=out_specs, check_vma=False)
```

```python
import functools
import math

import jax
import jax.numpy as jnp
import numpy as np
from jax import lax
from jax.experimental import pallas as pl
from jax.experimental.pallas import tpu as pltpu
from jax.sharding import Mesh
from jax.sharding import PartitionSpec as P

EPS = 0.006
ETA = 0.05
NEAR = ("x", "yl", "zl")
FAR = "zh"
SITE = ("yl", "zh", "zl", "x")
GRP = ("yh", "core")
EVERY = GRP + SITE
FINE = (2, 2, 2, 8, 2, 4)
LANES = 128
bf16, f32 = jnp.bfloat16, jnp.float32
VMEM = pl.BlockSpec(memory_space=pltpu.VMEM)
PARAMS = pltpu.CompilerParams(vmem_limit_bytes=40 * 2**20)


def halves(v):
    hi = v.astype(bf16).astype(f32)
    return hi, (v - hi).astype(bf16).astype(f32)


def lane_of(shape):
    return lax.broadcasted_iota(jnp.int32, shape, len(shape) - 1)


def left(v, by):
    return jnp.roll(v, -by, axis=-1) if v.shape[-1] < LANES else pltpu.roll(v, LANES - by, v.ndim - 1)


def partial_targets(n_near, noise, sites, weights, send, score_out):
    n_rows, width = noise.shape
    col = n_rows // n_near
    squares = jnp.zeros((sites.shape[0], LANES), f32)
    for c in range(0, width, LANES):
        part = sites[:, c : c + LANES].astype(f32)
        squares = squares + part * part
    half_sq = jnp.sum(squares.T, axis=0, keepdims=True) / (2.0 * width)
    inner = lax.dot_general(noise[...], sites[...], (((1,), (1,)), ((), ())), preferred_element_type=f32)
    score = weights[...] + (inner / width - half_sq) / EPS
    score_out[...] = score
    hi, low = halves(jnp.max(score, axis=1, keepdims=True))
    part = jnp.exp(score - (hi + low))
    stats = (hi, low) + halves(jnp.sum(part, axis=1, keepdims=True))
    lane = lane_of((col, LANES))
    tile = jnp.zeros((col, LANES), f32)
    for k in range(n_near):
        for p in range(4):
            tile = jnp.where(lane == 4 * k + p, stats[p][k * col : (k + 1) * col], tile)
    tile = tile.astype(bf16)
    for k in range(n_near):
        send[k * col : (k + 1) * col, width:] = tile
    send[:, :width] = jnp.dot(part.astype(bf16), sites[...], preferred_element_type=f32).astype(bf16)


def near_merge(n_near, own_k, got, out, stats):
    col, width = out.shape
    both = [got[s, :, width:].astype(f32) for s in range(n_near)]
    both = [v + left(v, 1) for v in both]
    first = lane_of((col, LANES)) % 4 == 0
    tops = [jnp.where(first, v, 0.0) for v in both]
    top = functools.reduce(jnp.maximum, tops)
    scales = [jnp.where(first, jnp.exp(v - top), 0.0) for v in tops]
    total = sum(c * jnp.where(first, left(v, 2), 0.0) for c, v in zip(scales, both))
    hi, low = halves(top)
    t_hi, t_low = halves(total)
    lane = lane_of((col, LANES)) % 4
    tile = jnp.where(lane == 0, hi, 0.0)
    for p, v in ((1, low), (2, t_hi), (3, t_low)):
        tile = jnp.where(lane == p, pltpu.roll(v, p, 1), tile)
    stats[...] = tile.astype(bf16)
    mine = lane_of((col, LANES)) == 4 * own_k[0]
    acc = jnp.zeros((col, width), f32)
    for s in range(n_near):
        c = jnp.sum(jnp.where(mine, scales[s], 0.0), axis=1, keepdims=True)
        acc = acc + c * got[s, :, :width].astype(f32)
    out[...] = acc.astype(bf16)


def normalise(n_near, all_sites, gain, at, stats, got, score, noise, weights, change, targets, potentials):
    n_far, col, _ = stats.shape
    own, width = noise.shape
    lane = lane_of((col, LANES))
    first = lane % 4 == 0
    both = [stats[s].astype(f32) for s in range(n_far)]
    both = [v + left(v, 1) for v in both]
    tops = [jnp.where(first, v, 0.0) for v in both]
    top = functools.reduce(jnp.maximum, tops)
    total = sum(jnp.where(first, jnp.exp(t - top) * left(v, 2), 1.0 / n_far) for t, v in zip(tops, both))
    lse = jnp.where(first, top + jnp.log(total), 0.0)
    acc = jnp.zeros((col, score.shape[1]), f32)
    for k in range(n_near):
        shift = jnp.sum(jnp.where(lane == 4 * k, lse, 0.0), axis=1, keepdims=True)
        acc = acc + jnp.exp(score[k * col : (k + 1) * col] - shift)
    change[...] = jnp.where(at[2] == 0, weights[...] + ETA, 0.0) - gain * jnp.sum(acc, axis=0, keepdims=True)

    sub = lax.broadcasted_iota(jnp.int32, (col, LANES), 0)
    here = [(sub == at[0] + r) & (lane == at[1]) for r in range(own)]
    row = lax.broadcasted_iota(jnp.int32, (own, 1), 0)

    def owned(v):
        picked = jnp.zeros((own, 1), f32)
        for r in range(own):
            value = jnp.sum(jnp.where(here[r], v, 0.0), axis=(0, 1), keepdims=True)
            picked = jnp.where(row == r, value, picked)
        return picked

    own_lse = owned(lse)
    total = jnp.zeros((own, width), f32)
    for s in range(n_far):
        total = total + jnp.exp(owned(tops[s]) - own_lse) * got[s, :, :width].astype(f32)
    targets[...] = total.astype(bf16)
    squares = noise[...].astype(f32)
    squares = jnp.sum(squares * squares, axis=1, keepdims=True)
    value = squares / (2.0 * width) - EPS * (own_lse - math.log(float(all_sites)))
    flat = jnp.zeros((1, LANES), f32)
    for r in range(own):
        flat = jnp.where(lane_of((1, LANES)) == r, value[r : r + 1], flat)
    potentials[...] = flat[:, :own]


LOOPS = np.arange(math.prod(FINE)).reshape(4, -1)[[0, 1, 3, 2]].T.tolist()


def run(kernel, outs, *args, first=None):
    specs = [VMEM] * len(args)
    if first is not None:
        args, specs = (first,) + args, [pl.BlockSpec(memory_space=pltpu.SMEM)] + specs
    return pl.pallas_call(
        kernel,
        out_shape=[jax.ShapeDtypeStruct(*o) for o in outs],
        in_specs=specs,
        out_specs=[VMEM] * len(outs),
        compiler_params=PARAMS,
    )(*args)


def exchange(v, axes):
    return lax.all_to_all(v, axes, 0, 0, tiled=True)


def spread(v, axes):
    return exchange(jnp.broadcast_to(v[None], (lax.axis_size(axes),) + v.shape), axes)


def gather_rows(noise):
    own, width = noise.shape
    rows = lax.all_gather(noise, ("zh", "zl"), axis=0)
    rows = rows.reshape(lax.axis_size("zh"), lax.axis_size("zl"), own, width)
    rows = jnp.transpose(rows, (1, 0, 2, 3)).reshape(-1, width)
    return spread(rows, ("x", "yl")).reshape(-1, width)


def shards(noise, sites, weights):
    own, width = noise.shape
    n_near, n_far = lax.axis_size(NEAR), lax.axis_size(FAR)
    col = n_far * own
    n_rows = n_near * col
    mine = sites.shape[0]
    all_sites = mine * lax.axis_size(SITE)
    all_rows = own * lax.axis_size(EVERY)
    own_k = lax.axis_index(NEAR)
    at = jnp.stack([lax.axis_index(FAR) * own, own_k * 4, lax.axis_index(GRP)])
    noise, own_k, at = lax.optimization_barrier((noise, own_k, at))
    rows = gather_rows(noise)
    send, score = run(
        functools.partial(partial_targets, n_near),
        [((n_rows, width + LANES), bf16), ((n_rows, mine), f32)],
        rows,
        sites,
        weights[None],
    )

    got = exchange(send.reshape(n_near, col, width + LANES), NEAR)
    part, stats = run(
        lambda k, *refs: near_merge(n_near, k, *refs),
        [((col, width), bf16), ((col, LANES), bf16)],
        got,
        first=own_k[None],
    )

    stats = stats[:, : 4 * n_near].reshape(own, -1)
    stats = jnp.broadcast_to(stats[None], (n_far,) + stats.shape)
    got = exchange(jnp.concatenate([part.reshape(n_far, own, width), stats], axis=2), FAR)
    stats = got[:, :, width:].reshape(n_far, col, 4 * n_near)
    stats = jnp.pad(stats, ((0, 0), (0, 0), (0, LANES - 4 * n_near)))
    gain = ETA * float(all_sites) / float(all_rows)
    change, targets, potentials = run(
        lambda at, *refs: normalise(n_near, all_sites, gain, at, *refs),
        [((1, mine), f32), ((own, width), bf16), ((1, own), f32)],
        stats,
        got,
        score,
        noise,
        weights[None],
        first=at,
    )
    return targets, potentials[0], lax.psum(change[0], EVERY, axis_index_groups=LOOPS)


def solution(mesh):
    fine = Mesh(np.asarray(mesh.devices).reshape(FINE), EVERY)
    in_specs = (P(EVERY, None), P(SITE, None), P(SITE))
    out_specs = (P(EVERY, None), P(EVERY), P(SITE))
    return jax.shard_map(shards, mesh=fine, in_specs=in_specs, out_specs=out_specs, check_vma=False)
```
